128 devices in a mesh: ma: 32 (over z, x, core), band: 4 (over y).
Axes of the slice: x: 4, y: 4, z: 4, core: 2. Of those that a mesh axis runs over, the one named last changes fastest.
Arguments:
- observed: bfloat16 [1024, 64, 1024], P(('ma', 'band')), may hold values from -6 to 6
- eigenvalues: float32 [1024, 1024], P(('ma', 'band')), may hold values from 0.05 to 20
- kl_basis: bfloat16 [1024, 1024, 512], P(('ma', 'band')), may hold values from -0.1875 to 0.1875
- band_deriv: bfloat16 [40, 512, 512], P('band'), may hold values from -0.15625 to 0.15625, as said below
- counts: int32 [1024], P(('ma', 'band')), may hold values from 128 to 1024, as said below
Outputs:
- mode_power: float32 [1024, 40], P('ma', 'band')
- band_power: float32 [40], P('band')
The draws below stay inside these ranges and needn't reach their ends.
Inputs may be any that keep to these rules, and one draw needn't show every extreme that they name: counts[m] is the number of leading KL modes of m-mode m that are kept; some m-mode keeps 1024 and some keeps 1024 // 8. Each band_deriv[a] is symmetric.
All inputs are finite; a program needn't handle non-finite values.
Results may differ from the reference program's by a relative error of at most 0.0018.
Values may be sent and summed in bfloat16 or wider, within the bound.
A program may use at most 64 MiB of HBM per device.

```python
import math
import jax
import jax.numpy as jnp
from jax import lax

BANDS = 40
W = 512
NMAX = 1024
S = 64
MTOT = 1024


def draw_band_deriv(key, part):
    gains = jnp.exp(jax.random.uniform(jax.random.fold_in(key, 11), (BANDS, W), jnp.float32, jnp.log(0.5), jnp.log(2.0)))
    raw = jax.random.normal(jax.random.fold_in(key, 12), (BANDS, W, W), jnp.float32)
    rough = jnp.clip((raw + jnp.transpose(raw, (0, 2, 1))) * 0.7071, -4.0, 4.0)
    identity = jnp.eye(W, dtype=jnp.float32)
    matrices = identity[None, :, :] * gains[:, :, None] + 1.5 * rough
    return (matrices * (4.0 / W)).astype(jnp.bfloat16)


def draw_counts(key, part):
    floor_count = NMAX // 8
    values = jax.random.randint(jax.random.fold_in(key, 21), (MTOT,), floor_count, NMAX + 1)
    first_slot = jax.random.randint(jax.random.fold_in(key, 22), (), 0, MTOT)
    second_slot = (first_slot + jax.random.randint(jax.random.fold_in(key, 23), (), 1, MTOT)) % MTOT
    values = values.at[first_slot].set(NMAX).at[second_slot].set(floor_count)
    return values.astype(jnp.int32)


def levels(key, dims, split, smallest, largest):
    gain, own = 1.0, jax.random.fold_in(key, 6)
    for axis_at, parts in split:
        draws = jnp.exp(jax.random.uniform(jax.random.fold_in(own, axis_at), (parts,), jnp.float32, smallest / len(split), largest / len(split)))
        gain = gain * jnp.repeat(draws, dims[axis_at] // parts).reshape([-1 if axis == axis_at else 1 for axis in range(len(dims))])
    return gain


def normal_values(own_key, dims, width, most, shards=(), kind=jnp.bfloat16):
    drawn = jax.random.normal(own_key, dims, jnp.float32) * width
    if len(shards) > 0:
        drawn = levels(own_key, dims, shards, -0.22, 0.18) * drawn
    return jnp.clip(drawn, min=-most, max=most).astype(kind)


def setup_inputs(seed: int = 0) -> dict:
    streams_of = jax.random.split(jax.random.key(seed), 6)
    observed = normal_values(streams_of[0], (MTOT, S, NMAX), 1.0, 6.0, ((0, 128),))
    eigenvalues = jnp.clip(jnp.exp(math.log(20.0) - 5.9914645 * jax.random.uniform(streams_of[1], (MTOT, NMAX), jnp.float32) ** levels(streams_of[1], (MTOT, NMAX), ((0, 128),), -0.2, 0.2)), 0.05, 20.0)
    kl_basis = normal_values(streams_of[2], (MTOT, NMAX, W), NMAX ** -0.5, 0.1875, ((0, 128),))
    band_deriv = draw_band_deriv(jax.random.fold_in(streams_of[5], 71), 0)
    counts = draw_counts(jax.random.fold_in(streams_of[5], 71), 0)
    return {"observed": observed, "eigenvalues": eigenvalues, "kl_basis": kl_basis, "band_deriv": band_deriv, "counts": counts}


def reference(observed, eigenvalues, kl_basis, band_deriv, counts):
    position = lax.broadcasted_iota(jnp.int32, eigenvalues.shape, 1)
    inside = position < counts[:, None]
    weights = jnp.where(inside, 1.0 / (1.0 + eigenvalues), jnp.zeros_like(eigenvalues))
    weighted = (observed.astype(jnp.float32) * weights[:, None, :]).astype(jnp.bfloat16)

    def project_one(operands):
        rows_block, basis_block = operands
        return jnp.dot(rows_block.astype(jnp.float32), basis_block.astype(jnp.float32)).astype(jnp.bfloat16)

    projected = lax.map(project_one, (weighted, kl_basis))
    flattened = projected.astype(jnp.float32).reshape(MTOT * S, W)

    def one_band(matrix):
        mapped = jnp.dot(flattened, matrix.astype(jnp.float32))
        return jnp.sum((mapped * flattened).reshape(MTOT, -1), axis=1)

    quadratic = lax.map(one_band, band_deriv)
    mode_power = jnp.transpose(quadratic) / S
    live_total = jnp.sum(counts).astype(jnp.float32)
    band_power = NMAX * jnp.sum(mode_power, axis=0) / live_total
    return mode_power, band_power
```

```python
import functools

import jax
import jax.numpy as jnp
from jax import lax
from jax.experimental import pallas as pl
from jax.experimental.pallas import tpu as pltpu
from jax.sharding import Mesh
from jax.sharding import PartitionSpec as P

MA = ("ma_0", "ma_1", "ma_2")
MA_BAND = MA + ("band",)
MESH = pl.DeviceIdType.MESH
LANES = 128
F32 = jnp.float32
BF16 = jnp.bfloat16


def kernel(
    counts_hbm, eig_hbm, obs_hbm, kl_hbm, d_hbm,
    mode_ref, power_ref,
    counts_s, eig_v, weight_v, obs_v, kl_v, d1_v, d2_v, vec, acc, tiles, row_c, rows,
    small_sem, obs_sem, kl_sem, d_sem, send_sem, recv_sem, csend_sem, crecv_sem, rsend_sem, rrecv_sem,
):
    own, samples, nmax = obs_v.shape
    bands, width, half = d1_v.shape
    depth = lax.axis_size("band")
    z, x, core = (lax.axis_index(a) for a in MA)
    nz, nx, nc = (lax.axis_size(a) for a in MA)
    plane = nz * nx * nc
    me = (z * nx + x) * nc + core
    y = lax.axis_index("band")
    right = lax.rem(y + 1, depth)
    left = lax.rem(y + depth - 1, depth)

    def peer(d):
        t = lax.rem(me + d, plane)
        return {"ma_0": t // (nx * nc), "ma_1": lax.rem(t // nc, nx), "ma_2": lax.rem(t, nc)}

    counts_cp = pltpu.make_async_copy(counts_hbm, counts_s, small_sem.at[0])
    eig_cp = pltpu.make_async_copy(eig_hbm, eig_v, small_sem.at[1])
    counts_cp.start()
    eig_cp.start()

    def obs_cp(m):
        return pltpu.make_async_copy(obs_hbm.at[m], obs_v.at[m], obs_sem.at[m])

    def kl_cp(m):
        return pltpu.make_async_copy(kl_hbm.at[m], kl_v.at[m], kl_sem.at[m])

    @pl.loop(0, own)
    def _(m):
        obs_cp(m).start()
        kl_cp(m).start()

    d1_cp = pltpu.make_async_copy(d_hbm.at[:, :, pl.ds(0, half)], d1_v, d_sem.at[0])
    d2_cp = pltpu.make_async_copy(d_hbm.at[:, pl.ds(half, half), pl.ds(half, half)], d2_v, d_sem.at[1])
    d1_cp.start()
    d2_cp.start()

    barrier = pltpu.get_barrier_semaphore()
    for n in (left, right):
        pl.semaphore_signal(barrier, inc=1, device_id={"band": n}, device_id_type=MESH)

    @pl.loop(1, plane)
    def _(d):
        pl.semaphore_signal(barrier, inc=1, device_id=peer(d), device_id_type=MESH)

    counts_cp.wait()
    eig_cp.wait()
    sub = lax.broadcasted_iota(jnp.int32, (own, nmax), 0)
    pos = lax.broadcasted_iota(jnp.int32, (own, nmax), 1)
    limit = jnp.zeros((own, nmax), jnp.int32)
    total = counts_s[0]
    for m in range(own):
        limit = jnp.where(sub == m, counts_s[m], limit)
        if m:
            total = total + counts_s[m]
    weight_v[...] = jnp.where(pos < limit, 1.0 / (1.0 + eig_v[...]), 0.0)
    row_c[0] = jnp.full((1, LANES), total.astype(F32))

    pl.semaphore_wait(barrier, plane + 1)

    def remote(src, dst, s, r, n):
        return pltpu.make_async_remote_copy(
            src_ref=src, dst_ref=dst, send_sem=s, recv_sem=r, device_id={"band": n}, device_id_type=MESH
        )

    def e_left(m):
        return 8 + (m // 4) * 8 + lax.rem(m, 4)

    def e_right(m):
        return 12 + (m // 4) * 8 + lax.rem(m, 4)

    def e_far_l(m):
        return 24 + (m // 2) * 4 + lax.rem(m, 2)

    def e_far_r(m):
        return 26 + (m // 2) * 4 + lax.rem(m, 2)

    def to_right(m):
        return remote(vec.at[m], vec.at[e_left(m)], send_sem.at[0, m], recv_sem.at[e_left(m)], right)

    def to_left(m):
        return remote(vec.at[m], vec.at[e_right(m)], send_sem.at[1, m], recv_sem.at[e_right(m)], left)

    def on_right(m):
        return remote(vec.at[e_left(m)], vec.at[e_far_l(m)], send_sem.at[0, 8 + m], recv_sem.at[e_far_l(m)], right)

    def on_left(m):
        e = e_right(m + 4)
        return remote(vec.at[e], vec.at[e_far_r(m)], send_sem.at[1, 8 + m], recv_sem.at[e_far_r(m)], left)

    def c_copy(s, d, k, n):
        return remote(row_c.at[s], row_c.at[d], csend_sem.at[k], crecv_sem.at[d], n)

    @pl.loop(0, own)
    def _(m):
        obs_cp(m).wait()
        kl_cp(m).wait()
        weighted = (obs_v[m].astype(F32) * weight_v[pl.ds(m, 1), :]).astype(BF16)
        vec[m] = jnp.dot(weighted, kl_v[m], preferred_element_type=F32).astype(BF16)
        to_right(m).start()
        to_left(m).start()

    c_copies = (c_copy(0, 1, 0, right), c_copy(0, 2, 1, left), c_copy(1, 3, 2, right))
    c_copies[0].start()
    c_copies[1].start()

    d1_cp.wait()
    d2_cp.wait()

    @pl.loop(0, bands)
    def _(a):
        d1_v[a, half:, :] = d1_v[a, half:, :] * 2

    def band_products(e0, n):
        @pl.loop(0, bands)
        def _(a):
            p = vec[e0 : e0 + n].reshape(n * samples, width)
            y1 = jnp.dot(p, d1_v[a], preferred_element_type=F32)
            y2 = jnp.dot(p[:, half:], d2_v[a], preferred_element_type=F32)
            q = y1 * p[:, :half].astype(F32) + y2 * p[:, half:].astype(F32)
            q = q[:, :LANES] + q[:, LANES:]
            q = jnp.sum(q.reshape(n, samples // 8, 8, LANES), axis=1)
            acc[a, e0 * 8 : (e0 + n) * 8, :] = q.reshape(n * 8, LANES)

    lane = lax.broadcasted_iota(jnp.int32, (8, LANES), 1)

    def gather_tile(g):
        t = jnp.zeros((8, LANES), F32)
        for a in range(bands):
            v = acc[a, pl.ds(g * 64, 8, stride=8), :]
            for k in range(1, 8):
                v = v + acc[a, pl.ds(g * 64 + k, 8, stride=8), :]
            t = jnp.where(lane == a, jnp.sum(v, axis=1, keepdims=True), t)
        t = t / samples
        tiles[g] = t

    band_products(0, 8)
    gather_tile(0)

    c_copies[0].wait_recv()
    c_copies[2].start()
    for m in range(4):
        to_right(m).wait_recv()
        on_right(m).start()
        to_left(m).wait_recv()
    band_products(8, 8)
    for m in range(4, 8):
        to_right(m).wait_recv()
        to_left(m).wait_recv()
        on_left(m - 4).start()
    gather_tile(1)
    band_products(16, 8)
    gather_tile(2)
    for q in range(2):
        for m in range(2 * q, 2 * q + 2):
            on_right(m).wait_recv()
            on_left(m).wait_recv()
        band_products(24 + 4 * q, 4)
    gather_tile(3)

    c_copies[1].wait_recv()
    c_copies[2].wait_recv()
    count = row_c[0] + row_c[1] + row_c[2] + row_c[3]
    part = jnp.sum(tiles[0] + tiles[1] + tiles[2] + tiles[3], axis=0, keepdims=True)
    lane1 = lax.broadcasted_iota(jnp.int32, (1, LANES), 1)
    rows[me] = jnp.where(lane1 == LANES - 1, count, part)

    def row_copy(d):
        return pltpu.make_async_remote_copy(
            src_ref=rows.at[me], dst_ref=rows.at[me], send_sem=rsend_sem, recv_sem=rrecv_sem,
            device_id=peer(d), device_id_type=MESH,
        )

    @pl.loop(1, plane)
    def _(d):
        row_copy(d).start()

    far = lax.rem(y + 2, depth)
    t1, t2, t3 = tiles[1], tiles[2], tiles[3]
    mode_ref[y] = tiles[0]
    mode_ref[left, 0:4, :] = t1[0:4]
    mode_ref[left, 4:8, :] = t2[0:4]
    mode_ref[right, 0:4, :] = t1[4:8]
    mode_ref[right, 4:8, :] = t2[4:8]
    mode_ref[far, 0:2, :] = t3[0:2]
    mode_ref[far, 4:6, :] = t3[2:4]
    mode_ref[far, 2:4, :] = t3[4:6]
    mode_ref[far, 6:8, :] = t3[6:8]

    for m in range(own):
        to_right(m).wait_send()
        to_left(m).wait_send()
    for m in range(4):
        on_right(m).wait_send()
        on_left(m).wait_send()
    for c in c_copies:
        c.wait_send()

    others = rows.at[pl.ds(0, plane - 1)]
    pltpu.make_async_copy(others, others, rrecv_sem).wait()
    pltpu.make_async_copy(others, others, rsend_sem).wait()
    whole = jnp.sum(rows[...].reshape(plane, LANES), axis=0, keepdims=True)
    live = jnp.sum(jnp.where(lane1 == LANES - 1, whole, 0.0), axis=1, keepdims=True)
    power_ref[...] = nmax * whole / live


def per_device(observed, eigenvalues, kl_basis, band_deriv, counts):
    own, samples, nmax = observed.shape
    bands, width, _ = band_deriv.shape
    half = width // 2
    depth = lax.axis_size("band")
    plane = lax.axis_size(MA)
    dma = pltpu.SemaphoreType.DMA
    mode, power = pl.pallas_call(
        kernel,
        out_shape=(
            jax.ShapeDtypeStruct((depth, own, LANES), F32),
            jax.ShapeDtypeStruct((1, LANES), F32),
        ),
        in_specs=[pl.BlockSpec(memory_space=pl.ANY)] * 5,
        out_specs=[pl.BlockSpec(memory_space=pltpu.VMEM)] * 2,
        scratch_shapes=[
            pltpu.SMEM((own,), jnp.int32),
            pltpu.VMEM((own, nmax), F32),
            pltpu.VMEM((own, nmax), F32),
            pltpu.VMEM((own, samples, nmax), BF16),
            pltpu.VMEM((own, nmax, width), BF16),
            pltpu.VMEM((bands, width, half), BF16),
            pltpu.VMEM((bands, half, half), BF16),
            pltpu.VMEM((depth * own, samples, width), BF16),
            pltpu.VMEM((bands, depth * own * 8, LANES), F32),
            pltpu.VMEM((depth, own, LANES), F32),
            pltpu.VMEM((depth, 1, LANES), F32),
            pltpu.VMEM((plane, 1, LANES), F32),
            dma((2,)),
            dma((own,)),
            dma((own,)),
            dma((2,)),
            dma((2, 12)),
            dma((32,)),
            dma((3,)),
            dma((4,)),
            dma,
            dma,
        ],
        compiler_params=pltpu.CompilerParams(
            collective_id=0, has_side_effects=True, vmem_limit_bytes=60 * 1024 * 1024
        ),
    )(counts, eigenvalues, observed, kl_basis, band_deriv)
    return mode.reshape(depth * own, LANES)[:, :bands], power[0, :bands]


def solution(mesh):
    split = Mesh(mesh.devices.reshape(4, 4, 2, mesh.shape["band"]), MA_BAND)
    return jax.shard_map(
        per_device,
        mesh=split,
        in_specs=(
            P(MA_BAND, None, None),
            P(MA_BAND, None),
            P(MA_BAND, None, None),
            P("band", None, None),
            P(MA_BAND),
        ),
        out_specs=(P(MA, "band"), P("band")),
        check_vma=False,
    )
```

```python
import functools

import jax
import jax.numpy as jnp
from jax import lax
from jax.experimental import pallas as pl
from jax.experimental.pallas import tpu as pltpu
from jax.sharding import Mesh
from jax.sharding import PartitionSpec as P

MA = ("ma_0", "ma_1", "ma_2")
MA_BAND = MA + ("band",)
MESH = pl.DeviceIdType.MESH
LANES = 128
F32 = jnp.float32
BF16 = jnp.bfloat16


def kernel(
    counts_hbm, eig_hbm, obs_hbm, kl_hbm, d_hbm,
    mode_ref, power_ref,
    counts_s, eig_v, weight_v, obs_v, kl_v, d1_v, d2_v, vec, acc, tiles, order, row_c, rows,
    small_sem, obs_sem, kl_sem, d_sem, send_sem, recv_sem, csend_sem, crecv_sem, rsend_sem, rrecv_sem, round_sem,
):
    own, samples, nmax = obs_v.shape
    bands, width, half = d1_v.shape
    depth = lax.axis_size("band")
    z, x, core = (lax.axis_index(a) for a in MA)
    nz, nx, nc = (lax.axis_size(a) for a in MA)
    plane = nz * nx * nc
    me = (z * nx + x) * nc + core
    y = lax.axis_index("band")
    right = lax.rem(y + 1, depth)
    left = lax.rem(y + depth - 1, depth)

    def peer(d):
        t = lax.rem(me + d, plane)
        return {"ma_0": t // (nx * nc), "ma_1": lax.rem(t // nc, nx), "ma_2": lax.rem(t, nc)}

    counts_cp = pltpu.make_async_copy(counts_hbm, counts_s, small_sem.at[0])
    eig_cp = pltpu.make_async_copy(eig_hbm, eig_v, small_sem.at[1])
    counts_cp.start()
    eig_cp.start()

    def obs_cp(m):
        return pltpu.make_async_copy(obs_hbm.at[m], obs_v.at[m], obs_sem.at[m])

    def kl_cp(m):
        return pltpu.make_async_copy(kl_hbm.at[m], kl_v.at[m], kl_sem.at[m])

    @pl.loop(0, own)
    def _(m):
        obs_cp(m).start()
        kl_cp(m).start()

    d1_cp = pltpu.make_async_copy(d_hbm.at[:, :, pl.ds(0, half)], d1_v, d_sem.at[0])
    d2_cp = pltpu.make_async_copy(d_hbm.at[:, pl.ds(half, half), pl.ds(half, half)], d2_v, d_sem.at[1])
    d1_cp.start()
    d2_cp.start()

    barrier = pltpu.get_barrier_semaphore()
    plane_near = []
    for axis, at, size in zip(MA, (z, x, core), (nz, nx, nc)):
        plane_near.append({axis: lax.rem(at + 1, size)})
        if size > 2:
            plane_near.append({axis: lax.rem(at + size - 1, size)})
    for n in [{"band": left}, {"band": right}] + plane_near:
        pl.semaphore_signal(barrier, inc=1, device_id=n, device_id_type=MESH)

    counts_cp.wait()
    eig_cp.wait()
    sub = lax.broadcasted_iota(jnp.int32, (own, nmax), 0)
    pos = lax.broadcasted_iota(jnp.int32, (own, nmax), 1)
    limit = jnp.zeros((own, nmax), jnp.int32)
    total = counts_s[0]
    for m in range(own):
        limit = jnp.where(sub == m, counts_s[m], limit)
        if m:
            total = total + counts_s[m]
    weight_v[...] = jnp.where(pos < limit, 1.0 / (1.0 + eig_v[...]), 0.0)
    row_c[0] = jnp.full((1, LANES), total.astype(F32))

    def pass_on(r):
        for n in plane_near:
            pl.semaphore_signal(round_sem.at[r], inc=1, device_id=n, device_id_type=MESH)

    def passed_on(r):
        pl.semaphore_wait(round_sem.at[r], len(plane_near))

    def remote(src, dst, s, r, n):
        return pltpu.make_async_remote_copy(
            src_ref=src, dst_ref=dst, send_sem=s, recv_sem=r, device_id={"band": n}, device_id_type=MESH
        )

    def e_left(m):
        return 8 + (m // 4) * 8 + lax.rem(m, 4)

    def e_right(m):
        return 12 + (m // 4) * 8 + lax.rem(m, 4)

    def e_far_l(m):
        return 24 + (m // 2) * 4 + lax.rem(m, 2)

    def e_far_r(m):
        return 26 + (m // 2) * 4 + lax.rem(m, 2)

    def to_right(m):
        return remote(vec.at[m], vec.at[e_left(m)], send_sem.at[0, m], recv_sem.at[e_left(m)], right)

    def to_left(m):
        return remote(vec.at[m], vec.at[e_right(m)], send_sem.at[1, m], recv_sem.at[e_right(m)], left)

    def on_right(m):
        return remote(vec.at[e_left(m)], vec.at[e_far_l(m)], send_sem.at[0, 8 + m], recv_sem.at[e_far_l(m)], right)

    def on_left(m):
        e = e_right(m + 4)
        return remote(vec.at[e], vec.at[e_far_r(m)], send_sem.at[1, 8 + m], recv_sem.at[e_far_r(m)], left)

    def c_copy(s, d, k, n):
        return remote(row_c.at[s], row_c.at[d], csend_sem.at[k], crecv_sem.at[d], n)

    def project(m):
        obs_cp(m).wait()
        kl_cp(m).wait()
        weighted = (obs_v[m].astype(F32) * weight_v[pl.ds(m, 1), :]).astype(BF16)
        vec[m] = jnp.dot(weighted, kl_v[m], preferred_element_type=F32).astype(BF16)

    project(0)
    pl.semaphore_wait(barrier, 2 + len(plane_near))
    to_right(0).start()
    to_left(0).start()
    pass_on(0)

    @pl.loop(1, own)
    def _(m):
        project(m)
        to_right(m).start()
        to_left(m).start()

    passed_on(0)
    pass_on(1)
    c_copies = (c_copy(0, 1, 0, right), c_copy(0, 2, 1, left), c_copy(1, 3, 2, right))
    c_copies[0].start()
    c_copies[1].start()

    d1_cp.wait()
    d2_cp.wait()

    @pl.loop(0, bands)
    def _(a):
        d1_v[a, half:, :] = d1_v[a, half:, :] * 2

    def band_products(e0, n):
        @pl.loop(0, bands // 5)
        def _(step):
          for u in range(5):
            a = step * 5 + u
            p = vec[e0 : e0 + n].reshape(n * samples, width)
            y1 = jnp.dot(p, d1_v[a], preferred_element_type=F32)
            y2 = jnp.dot(p[:, half:], d2_v[a], preferred_element_type=F32)
            q = y1 * p[:, :half].astype(F32) + y2 * p[:, half:].astype(F32)
            q = q[:, :LANES] + q[:, LANES:]
            q = jnp.sum(q.reshape(n, samples // 8, 8, LANES), axis=1)
            acc[a, e0 * 8 : (e0 + n) * 8, :] = q.reshape(n * 8, LANES)

    lane = lax.broadcasted_iota(jnp.int32, (8, LANES), 1)

    def gather_tile(g):
        t = jnp.zeros((8, LANES), F32)
        for a in range(bands):
            v = acc[a, pl.ds(g * 64, 8, stride=8), :]
            for k in range(1, 8):
                v = v + acc[a, pl.ds(g * 64 + k, 8, stride=8), :]
            t = jnp.where(lane == a, jnp.sum(v, axis=1, keepdims=True), t)
        t = t / samples
        tiles[g] = t

    band_products(0, 8)
    passed_on(1)
    pass_on(2)
    gather_tile(0)

    c_copies[0].wait_recv()
    c_copies[2].start()
    for m in range(4):
        to_right(m).wait_recv()
        on_right(m).start()
        to_left(m).wait_recv()
    band_products(8, 8)
    passed_on(2)
    pass_on(3)
    for m in range(4, 8):
        to_right(m).wait_recv()
        to_left(m).wait_recv()
        on_left(m - 4).start()
    gather_tile(1)
    band_products(16, 8)
    passed_on(3)
    gather_tile(2)
    for q in range(2):
        for m in range(2 * q, 2 * q + 2):
            on_right(m).wait_recv()
            on_left(m).wait_recv()
        band_products(24 + 4 * q, 4)
    gather_tile(3)

    c_copies[1].wait_recv()
    c_copies[2].wait_recv()
    count = row_c[0] + row_c[1] + row_c[2] + row_c[3]
    part = jnp.sum(tiles[0] + tiles[1] + tiles[2] + tiles[3], axis=0, keepdims=True)
    lane1 = lax.broadcasted_iota(jnp.int32, (1, LANES), 1)
    rows[me] = jnp.where(lane1 == LANES - 1, count, part)

    def row_copy(d):
        return pltpu.make_async_remote_copy(
            src_ref=rows.at[me], dst_ref=rows.at[me], send_sem=rsend_sem, recv_sem=rrecv_sem,
            device_id=peer(d), device_id_type=MESH,
        )

    @pl.loop(1, plane)
    def _(d):
        row_copy(d).start()

    far = lax.rem(y + 2, depth)
    t1, t2, t3 = tiles[1], tiles[2], tiles[3]
    order[y] = tiles[0]
    order[left, 0:4, :] = t1[0:4]
    order[left, 4:8, :] = t2[0:4]
    order[right, 0:4, :] = t1[4:8]
    order[right, 4:8, :] = t2[4:8]
    order[far, 0:2, :] = t3[0:2]
    order[far, 4:6, :] = t3[2:4]
    order[far, 2:4, :] = t3[4:6]
    order[far, 6:8, :] = t3[6:8]
    mode_ref[...] = jnp.transpose(order[...].reshape(depth * own, LANES))[0:bands, :]

    for m in range(own):
        to_right(m).wait_send()
        to_left(m).wait_send()
    for m in range(4):
        on_right(m).wait_send()
        on_left(m).wait_send()
    for c in c_copies:
        c.wait_send()

    others = rows.at[pl.ds(0, plane - 1)]
    pltpu.make_async_copy(others, others, rrecv_sem).wait()
    pltpu.make_async_copy(others, others, rsend_sem).wait()
    whole = jnp.sum(rows[...].reshape(plane, LANES), axis=0, keepdims=True)
    live = jnp.sum(jnp.where(lane1 == LANES - 1, whole, 0.0), axis=1, keepdims=True)
    power_ref[...] = nmax * whole / live


def results(mode_ref, power_ref, mode_out, power_out):
    mode_out[...] = mode_ref[...]
    power_out[...] = power_ref[0, : power_out.shape[0]]


def per_device(observed, eigenvalues, kl_basis, band_deriv, counts):
    own, samples, nmax = observed.shape
    bands, width, _ = band_deriv.shape
    half = width // 2
    depth = lax.axis_size("band")
    plane = lax.axis_size(MA)
    dma = pltpu.SemaphoreType.DMA
    mode, power = pl.pallas_call(
        kernel,
        out_shape=(
            jax.ShapeDtypeStruct((bands, depth * own), F32),
            jax.ShapeDtypeStruct((1, LANES), F32),
        ),
        in_specs=[pl.BlockSpec(memory_space=pltpu.HBM)] * 5,
        out_specs=[pl.BlockSpec(memory_space=pltpu.VMEM)] * 2,
        scratch_shapes=[
            pltpu.SMEM((own,), jnp.int32),
            pltpu.VMEM((own, nmax), F32),
            pltpu.VMEM((own, nmax), F32),
            pltpu.VMEM((own, samples, nmax), BF16),
            pltpu.VMEM((own, nmax, width), BF16),
            pltpu.VMEM((bands, width, half), BF16),
            pltpu.VMEM((bands, half, half), BF16),
            pltpu.VMEM((depth * own, samples, width), BF16),
            pltpu.VMEM((bands, depth * own * 8, LANES), F32),
            pltpu.VMEM((depth, own, LANES), F32),
            pltpu.VMEM((depth, own, LANES), F32),
            pltpu.VMEM((depth, 1, LANES), F32),
            pltpu.VMEM((plane, 1, LANES), F32),
            dma((2,)),
            dma((own,)),
            dma((own,)),
            dma((2,)),
            dma((2, 12)),
            dma((32,)),
            dma((3,)),
            dma((4,)),
            dma,
            dma,
            pltpu.SemaphoreType.REGULAR((4,)),
        ],
        compiler_params=pltpu.CompilerParams(
            collective_id=0, has_side_effects=True, vmem_limit_bytes=63 * 1024 * 1024
        ),
    )(counts, eigenvalues, observed, kl_basis, band_deriv)
    mode, power = pl.pallas_call(
        results,
        out_shape=(jax.ShapeDtypeStruct(mode.shape, F32), jax.ShapeDtypeStruct((bands,), F32)),
    )(mode, power)
    return mode.T, power


def solution(mesh):
    split = Mesh(mesh.devices.reshape(4, 4, 2, mesh.shape["band"]), MA_BAND)
    return jax.shard_map(
        per_device,
        mesh=split,
        in_specs=(
            P(MA_BAND, None, None),
            P(MA_BAND, None),
            P(MA_BAND, None, None),
            P("band", None, None),
            P(MA_BAND),
        ),
        out_specs=(P(MA, "band"), P("band")),
        check_vma=False,
    )
```

```python
import functools

import jax
import jax.numpy as jnp
from jax import lax
from jax.experimental import pallas as pl
from jax.experimental.pallas import tpu as pltpu
from jax.sharding import Mesh
from jax.sharding import PartitionSpec as P

MA = ("ma_0", "ma_1", "ma_2")
MA_BAND = MA + ("band",)
MESH = pl.DeviceIdType.MESH
LANES = 128
F32 = jnp.float32
BF16 = jnp.bfloat16
FAR = ((0, 4), (4, 6), (6, 8))


def kernel(
    counts_hbm, eig_hbm, obs_hbm, kl_hbm, d_hbm,
    mode_ref, power_ref,
    counts_s, eig_v, weight_v, obs_v, kl_v, d1_v, d2_v, vec, acc, tiles, order, row_c, rows,
    small_sem, load_sem, d_sem, send_sem, recv_sem, far_sem, csend_sem, crecv_sem, rsend_sem, rrecv_sem, round_sem,
):
    own, samples, nmax = obs_v.shape
    bands, width, half = d1_v.shape
    depth = lax.axis_size("band")
    z, x, core = (lax.axis_index(a) for a in MA)
    nz, nx, nc = (lax.axis_size(a) for a in MA)
    plane = nz * nx * nc
    me = (z * nx + x) * nc + core
    y = lax.axis_index("band")
    right = lax.rem(y + 1, depth)
    left = lax.rem(y + depth - 1, depth)

    def obs_cp(m):
        return pltpu.make_async_copy(obs_hbm.at[m], obs_v.at[m], load_sem.at[2 * m])

    def kl_cp(m):
        return pltpu.make_async_copy(kl_hbm.at[m], kl_v.at[m], load_sem.at[2 * m + 1])

    counts_cp = pltpu.make_async_copy(counts_hbm, counts_s, small_sem.at[0])
    eig_cp = pltpu.make_async_copy(eig_hbm, eig_v, small_sem.at[1])
    counts_cp.start()
    kl_cp(0).start()
    obs_cp(0).start()
    eig_cp.start()

    @pl.loop(1, own)
    def _(m):
        obs_cp(m).start()
        kl_cp(m).start()

    d1_cp = pltpu.make_async_copy(d_hbm.at[:, :, pl.ds(0, half)], d1_v, d_sem.at[0])
    d2_cp = pltpu.make_async_copy(d_hbm.at[:, pl.ds(half, half), pl.ds(half, half)], d2_v, d_sem.at[1])
    d1_cp.start()
    d2_cp.start()

    barrier = pltpu.get_barrier_semaphore()
    plane_near = []
    for axis, at, size in zip(MA, (z, x, core), (nz, nx, nc)):
        plane_near.append({axis: lax.rem(at + 1, size)})
        if size > 2:
            plane_near.append({axis: lax.rem(at + size - 1, size)})
    for n in [{"band": left}, {"band": right}] + plane_near:
        pl.semaphore_signal(barrier, inc=1, device_id=n, device_id_type=MESH)

    counts_cp.wait()
    eig_cp.wait()
    sub = lax.broadcasted_iota(jnp.int32, (own, nmax), 0)
    pos = lax.broadcasted_iota(jnp.int32, (own, nmax), 1)
    limit = jnp.zeros((own, nmax), jnp.int32)
    total = counts_s[0]
    for m in range(own):
        limit = jnp.where(sub == m, counts_s[m], limit)
        if m:
            total = total + counts_s[m]
    weight_v[...] = jnp.where(pos < limit, 1.0 / (1.0 + eig_v[...]), 0.0)
    row_c[0] = jnp.full((1, LANES), total.astype(F32))

    def pass_on(r):
        for n in plane_near:
            pl.semaphore_signal(round_sem.at[r], inc=1, device_id=n, device_id_type=MESH)

    def passed_on(r):
        pl.semaphore_wait(round_sem.at[r], len(plane_near))

    def remote(src, dst, s, r, n):
        return pltpu.make_async_remote_copy(
            src_ref=src, dst_ref=dst, send_sem=s, recv_sem=r, device_id={"band": n}, device_id_type=MESH
        )

    def e_left(m):
        return 8 + (m // 2) * 4 + lax.rem(m, 2)

    def e_right(m):
        return 10 + (m // 2) * 4 + lax.rem(m, 2)

    def to_right(m):
        return remote(vec.at[m], vec.at[e_left(m)], send_sem, recv_sem.at[0, m // 2], right)

    def to_left(m):
        return remote(vec.at[m], vec.at[e_right(m)], send_sem, recv_sem.at[1, m // 2], left)

    def on_right(m, step):
        src = vec.at[e_left(m), pl.ds(0, samples // 2)]
        return remote(src, vec.at[24 + m, pl.ds(0, samples // 2)], send_sem, far_sem.at[step], right)

    def on_left(m, step):
        rest = pl.ds(samples // 2, samples // 2)
        return remote(vec.at[e_right(m), rest], vec.at[24 + m, rest], send_sem, far_sem.at[step], left)

    def arrived(e, n, sem):
        landed = vec.at[pl.ds(e, n)]
        pltpu.make_async_copy(landed, landed, sem).wait()

    def c_copy(s, d, k, n):
        return remote(row_c.at[s], row_c.at[d], csend_sem, crecv_sem.at[k], n)

    def project(m):
        obs_cp(m).wait()
        kl_cp(m).wait()
        weighted = (obs_v[m].astype(F32) * weight_v[pl.ds(m, 1), :]).astype(BF16)
        vec[m] = jnp.dot(weighted, kl_v[m], preferred_element_type=F32).astype(BF16)

    project(0)
    pl.semaphore_wait(barrier, 2 + len(plane_near))
    c_copies = (c_copy(0, 1, 0, right), c_copy(0, 2, 1, left), c_copy(1, 3, 1, right))
    c_copies[0].start()
    c_copies[1].start()
    to_right(0).start()
    to_left(0).start()
    pass_on(0)

    @pl.loop(1, own)
    def _(m):
        project(m)
        to_right(m).start()
        to_left(m).start()

    d1_cp.wait()
    d2_cp.wait()

    @pl.loop(0, bands)
    def _(a):
        d1_v[a, half:, :] = d1_v[a, half:, :] * 2

    def band_products(e0, n):
        unroll = bands if n <= 2 else 5

        @pl.loop(0, bands // unroll)
        def _(step):
          for u in range(unroll):
            a = step * unroll + u
            p = vec[e0 : e0 + n].reshape(n * samples, width)
            y1 = jnp.dot(p, d1_v[a], preferred_element_type=F32)
            y2 = jnp.dot(p[:, half:], d2_v[a], preferred_element_type=F32)
            q = y1 * p[:, :half].astype(F32) + y2 * p[:, half:].astype(F32)
            q = q[:, :LANES] + q[:, LANES:]
            q = jnp.sum(q.reshape(n, samples // 8, 8, LANES), axis=1)
            acc[a, e0 * 8 : (e0 + n) * 8, :] = q.reshape(n * 8, LANES)

    lane = lax.broadcasted_iota(jnp.int32, (8, LANES), 1)

    def gather_tile(g):
        t = jnp.zeros((8, LANES), F32)
        for a in range(bands):
            v = acc[a, pl.ds(g * 64, 8, stride=8), :]
            for k in range(1, 8):
                v = v + acc[a, pl.ds(g * 64 + k, 8, stride=8), :]
            t = jnp.where(lane == a, jnp.sum(v, axis=1, keepdims=True), t)
        tiles[g] = t / samples

    step_of = {m: i for i, (m0, m1) in enumerate(FAR) for m in range(m0, m1)}

    def from_both(pair):
        modes = (2 * pair, 2 * pair + 1)
        arrived(8 + 4 * pair, 2, recv_sem.at[0, pair])
        for m in modes:
            on_right(m, step_of[m]).start()
        arrived(10 + 4 * pair, 2, recv_sem.at[1, pair])
        for m in modes:
            on_left(m, step_of[m]).start()

    band_products(0, 8)
    passed_on(0)
    pass_on(1)
    gather_tile(0)
    from_both(0)
    from_both(1)
    band_products(8, 8)
    passed_on(1)
    pass_on(2)
    c_copies[0].wait_recv()
    c_copies[2].start()
    gather_tile(1)
    from_both(2)
    band_products(16, 4)
    from_both(3)
    passed_on(2)
    pass_on(3)
    band_products(20, 4)
    gather_tile(2)
    near = tiles[0] + tiles[1] + tiles[2]
    for step, (m0, m1) in enumerate(FAR):
        arrived(24 + m0, m1 - m0, far_sem.at[step])
        band_products(24 + m0, m1 - m0)
    gather_tile(3)
    passed_on(3)

    rest_c = row_c.at[pl.ds(2, 2)]
    pltpu.make_async_copy(rest_c, rest_c, crecv_sem.at[1]).wait()
    count = row_c[0] + row_c[1] + row_c[2] + row_c[3]
    part = jnp.sum(near + tiles[3], axis=0, keepdims=True)
    lane1 = lax.broadcasted_iota(jnp.int32, (1, LANES), 1)
    rows[me] = jnp.where(lane1 == LANES - 1, count, part)

    shifts = [(a, b, c) for a in range(nz) for b in range(nx) for c in range(nc)]
    shifts.sort(key=lambda s: -(min(s[0], nz - s[0]) + min(s[1], nx - s[1])))
    zs, xs, cs = ([lax.rem(at + i, n) for i in range(n)] for at, n in ((z, nz), (x, nx), (core, nc)))
    for a, b, c in shifts:
        if a or b or c:
            pltpu.make_async_remote_copy(
                src_ref=rows.at[me], dst_ref=rows.at[me], send_sem=rsend_sem, recv_sem=rrecv_sem,
                device_id=dict(zip(MA, (zs[a], xs[b], cs[c]))), device_id_type=MESH,
            ).start()

    far = lax.rem(y + 2, depth)
    order[y] = tiles[0]
    for c in range(2):
        t = tiles[1 + c]
        order[left, 4 * c : 4 * c + 2, :] = t[0:2]
        order[left, 4 * c + 2 : 4 * c + 4, :] = t[4:6]
        order[right, 4 * c : 4 * c + 2, :] = t[2:4]
        order[right, 4 * c + 2 : 4 * c + 4, :] = t[6:8]
    order[far] = tiles[3]
    mode_ref[...] = jnp.transpose(order[...].reshape(depth * own, LANES))[0:bands, :]

    sent = vec.at[pl.ds(0, 3 * own)]
    pltpu.make_async_copy(sent, sent, send_sem).wait()
    rows_c = row_c.at[pl.ds(0, 3)]
    pltpu.make_async_copy(rows_c, rows_c, csend_sem).wait()
    others = rows.at[pl.ds(0, plane - 1)]
    pltpu.make_async_copy(others, others, rsend_sem).wait()
    pltpu.make_async_copy(others, others, rrecv_sem).wait()
    whole = jnp.sum(rows[...].reshape(plane, LANES), axis=0, keepdims=True)
    live = jnp.sum(jnp.where(lane1 == LANES - 1, whole, 0.0), axis=1, keepdims=True)
    power_ref[...] = (nmax * whole / live)[0, :bands]


def results(mode_ref, power_ref, mode_out, power_out, sems):
    copies = (
        pltpu.make_async_copy(mode_ref, mode_out, sems.at[0]),
        pltpu.make_async_copy(power_ref, power_out, sems.at[1]),
    )
    for c in copies:
        c.start()
    for c in copies:
        c.wait()


def per_device(observed, eigenvalues, kl_basis, band_deriv, counts):
    own, samples, nmax = observed.shape
    bands, width, _ = band_deriv.shape
    half = width // 2
    depth = lax.axis_size("band")
    plane = lax.axis_size(MA)
    dma = pltpu.SemaphoreType.DMA
    counts, eigenvalues, observed, kl_basis, band_deriv = (
        pltpu.with_memory_space_constraint(v, pltpu.HBM)
        for v in (counts, eigenvalues, observed, kl_basis, band_deriv)
    )
    mode, power = pl.pallas_call(
        kernel,
        out_shape=(
            jax.ShapeDtypeStruct((bands, depth * own), F32),
            jax.ShapeDtypeStruct((bands,), F32),
        ),
        in_specs=[pl.BlockSpec(memory_space=pltpu.HBM)] * 5,
        out_specs=[pl.BlockSpec(memory_space=pltpu.VMEM)] * 2,
        scratch_shapes=[
            pltpu.SMEM((own,), jnp.int32),
            pltpu.VMEM((own, nmax), F32),
            pltpu.VMEM((own, nmax), F32),
            pltpu.VMEM((own, samples, nmax), BF16),
            pltpu.VMEM((own, nmax, width), BF16),
            pltpu.VMEM((bands, width, half), BF16),
            pltpu.VMEM((bands, half, half), BF16),
            pltpu.VMEM((depth * own, samples, width), BF16),
            pltpu.VMEM((bands, depth * own * 8, LANES), F32),
            pltpu.VMEM((depth, own, LANES), F32),
            pltpu.VMEM((depth, own, LANES), F32),
            pltpu.VMEM((depth, 1, LANES), F32),
            pltpu.VMEM((plane, 1, LANES), F32),
            dma((2,)),
            dma((2 * own,)),
            dma((2,)),
            dma,
            dma((2, own // 2)),
            dma((len(FAR),)),
            dma,
            dma((2,)),
            dma,
            dma,
            pltpu.SemaphoreType.REGULAR((4,)),
        ],
        compiler_params=pltpu.CompilerParams(
            collective_id=0, has_side_effects=True, vmem_limit_bytes=50 * 1024 * 1024
        ),
    )(counts, eigenvalues, observed, kl_basis, band_deriv)
    mode, power = (pltpu.with_memory_space_constraint(v, pltpu.VMEM) for v in (mode, power))
    mode, power = pl.pallas_call(
        results,
        out_shape=(jax.ShapeDtypeStruct(mode.shape, F32), jax.ShapeDtypeStruct(power.shape, F32)),
        in_specs=[pl.BlockSpec(memory_space=pltpu.VMEM)] * 2,
        out_specs=[pl.BlockSpec(memory_space=pl.ANY)] * 2,
        scratch_shapes=[dma((2,))],
    )(mode, power)
    return mode.T, power


def solution(mesh):
    split = Mesh(mesh.devices.reshape(4, 4, 2, mesh.shape["band"]), MA_BAND)
    return jax.shard_map(
        per_device,
        mesh=split,
        in_specs=(
            P(MA_BAND, None, None),
            P(MA_BAND, None),
            P(MA_BAND, None, None),
            P("band", None, None),
            P(MA_BAND),
        ),
        out_specs=(P(MA, "band"), P("band")),
        check_vma=False,
    )
```
